32 devices in a mesh: space: 16 (over z, y, core), grp: 2 (over x).
Axes of the slice: x: 2, y: 2, z: 4, core: 2. Of those that a mesh axis runs over, the one named last changes fastest.
Arguments:
- diag_blocks: float32 [16, 2, 128, 128], P('space', 'grp'), may hold values from -0.4 to 0.4
- x_coupling: float32 [16, 2, 128, 128], P('space', 'grp'), may hold values from -0.35 to 0.35
- y_coupling: float32 [16, 2, 128, 128], P('space', 'grp'), may hold values from -0.35 to 0.35
- levels: float32 [16, 2, 128], P('space', 'grp'), may hold values from -2 to 2
- listed: int32 [16, 2, 2], P('space', 'grp'), may hold values 0 or 1
Outputs:
- density_diag: float32 [16, 2, 128, 128], P('space', 'grp')
- density_x: float32 [16, 2, 128, 128], P('space', 'grp')
- density_y: float32 [16, 2, 128, 128], P('space', 'grp')
The draws below stay inside these ranges and needn't reach their ends.
Inputs may be any that keep to these rules, and one draw needn't show every extreme that they name: listed[i,j,0] keeps the coupling of block (i,j) with (i+1,j), listed[i,j,1] that with (i,j+1).
All inputs are finite; a program needn't handle non-finite values.
Results may differ from the reference program's by a relative error of at most 0.0037.
Values sent between devices are 32-bit elements; how exact they have to be, the bound alone decides.
A program may use at most 64 MiB of HBM per device.

```python
import jax
import jax.numpy as jnp
from jax import lax

BLK = 128
NX = 16
NY = 2


def set_ends(entries, stream_key, low, largest):
    dims = entries.shape
    place = [jax.random.randint(jax.random.fold_in(stream_key, axis), (), 0, dims[axis]) for axis in range(len(dims))]
    entries = entries.at[tuple(place)].set(low)
    longest = dims.index(max(dims))
    place[longest] = (place[longest] + 1) % dims[longest]
    return entries.at[tuple(place)].set(largest)


def steps_of(stream_key, shape, shards, low, top_value):
    factor_of, own = 1.0, jax.random.fold_in(stream_key, 6)
    for position, shards_of in shards:
        draws = jnp.exp(jax.random.uniform(jax.random.fold_in(own, position), (shards_of,), jnp.float32, low / len(shards), top_value / len(shards)))
        factor_of = factor_of * jnp.repeat(draws, shape[position] // shards_of).reshape([-1 if axis == position else 1 for axis in range(len(shape))])
    return factor_of


def normal_values(own_key, dims, deviation, limit, shards=(), kind=jnp.bfloat16):
    loudness = steps_of(own_key, dims, shards, -0.22, 0.18) if shards else 1.0
    values = jax.random.normal(own_key, dims, jnp.float32) * deviation * loudness
    return jnp.minimum(jnp.maximum(values, -limit), limit).astype(kind)


def setup_inputs(seed: int = 0) -> dict:
    seeds = jax.random.split(jax.random.key(seed), 6)
    diag_blocks = normal_values(seeds[0], (NX, NY, BLK, BLK), 0.06, 0.4, ((0, 16), (1, 2)), jnp.float32)
    x_coupling = normal_values(seeds[1], (NX, NY, BLK, BLK), 0.05, 0.35, ((0, 16), (1, 2)), jnp.float32)
    y_coupling = normal_values(seeds[2], (NX, NY, BLK, BLK), 0.05, 0.35, ((0, 16), (1, 2)), jnp.float32)
    levels = jnp.clip(jax.random.uniform(seeds[3], (NX, NY, BLK), jnp.float32, -2.0, 2.0) * steps_of(seeds[3], (NX, NY, BLK), ((0, 16), (1, 2)), -0.4, 0.0), -2.0, 2.0)
    listed = set_ends((jax.random.randint(seeds[4], (NX, NY, 2), 0, 4) < 3).astype(jnp.int32), jax.random.fold_in(seeds[4], 1), 0, 1)
    return {"diag_blocks": diag_blocks, "x_coupling": x_coupling, "y_coupling": y_coupling, "levels": levels, "listed": listed}


hubbard = 1.0

def symmetric(matrix):
    return 0.5 * (matrix + matrix.T)

def assemble(center, nbr_diag, nbr_coup):
    block_width = center.shape[0]
    zero_block = jnp.zeros((block_width, block_width), center.dtype)
    top_row = jnp.concatenate([center] + [nbr_coup[member].T for member in range(4)], axis=1)
    row_list = [top_row]
    for member in range(4):
        pieces = [nbr_coup[member]] + [nbr_diag[member] if column_slot == member else zero_block for column_slot in range(4)]
        row_list.append(jnp.concatenate(pieces, axis=1))
    return jnp.concatenate(row_list, axis=0)

def density_column(matrix):
    order_size = matrix.shape[0]
    block_width = order_size // 5
    matrix_half = matrix.astype(jnp.bfloat16)
    square = jnp.dot(matrix_half, matrix_half, preferred_element_type=jnp.float32)
    square_half = square.astype(jnp.bfloat16)
    fourth = jnp.dot(square_half, square_half, preferred_element_type=jnp.float32)
    scale_four = jnp.sqrt(jnp.sum(fourth * fourth) + 1e-06)
    scale_two = jnp.sqrt(scale_four)
    scale_one = jnp.sqrt(scale_two)
    identity = jnp.eye(order_size, dtype=jnp.float32)
    initial = (matrix / scale_one).astype(jnp.bfloat16)
    factor = (3.0 * identity - square / scale_two).astype(jnp.bfloat16)
    iterate = (0.5 * jnp.dot(initial, factor, preferred_element_type=jnp.float32)).astype(jnp.bfloat16)
    column = iterate[:, :block_width]
    applied_once = jnp.dot(iterate, column, preferred_element_type=jnp.float32).astype(jnp.bfloat16)
    applied_twice = jnp.dot(iterate, applied_once, preferred_element_type=jnp.float32)
    sign_part = 0.5 * (3.0 * column.astype(jnp.float32) - applied_twice)
    density = 0.5 * (identity[:, :block_width] - sign_part)
    return density.reshape(5, block_width, block_width)

def sweep(diag_all, x_all, y_all):
    size_x = diag_all.shape[0]
    size_y = diag_all.shape[1]
    block_width = diag_all.shape[2]
    widths = ((1, 1), (1, 1), (0, 0), (0, 0))
    pad_diag = jnp.pad(diag_all, widths)
    pad_x = jnp.pad(x_all, widths)
    pad_y = jnp.pad(y_all, widths)
    zero_index = jnp.int32(0)

    def one_site(flat):
        row_index = flat // size_y
        col_index = flat % size_y

        def pick(array, shift_x, shift_y):
            start_x = (row_index + (1 + shift_x)).astype(jnp.int32)
            start_y = (col_index + (1 + shift_y)).astype(jnp.int32)
            return lax.dynamic_slice(array, (start_x, start_y, zero_index, zero_index), (1, 1, block_width, block_width))[0, 0]
        center = pick(pad_diag, 0, 0)
        nbr_diag = jnp.stack([pick(pad_diag, -1, 0), pick(pad_diag, 1, 0), pick(pad_diag, 0, -1), pick(pad_diag, 0, 1)])
        nbr_coup = jnp.stack([pick(pad_x, -1, 0), pick(pad_x, 0, 0).T, pick(pad_y, 0, -1), pick(pad_y, 0, 0).T])
        return density_column(assemble(center, nbr_diag, nbr_coup))
    columns = lax.map(one_site, jnp.arange(size_x * size_y, dtype=jnp.int32))
    columns = columns.reshape(size_x, size_y, 5, block_width, block_width)
    diag_density = 0.5 * (columns[:, :, 0] + jnp.swapaxes(columns[:, :, 0], -1, -2))
    from_x = jnp.concatenate([columns[1:, :, 1], jnp.zeros_like(columns[:1, :, 1])], axis=0)
    x_density = 0.5 * (jnp.swapaxes(columns[:, :, 2], -1, -2) + from_x)
    from_y = jnp.concatenate([columns[:, 1:, 3], jnp.zeros_like(columns[:, :1, 3])], axis=1)
    y_density = 0.5 * (jnp.swapaxes(columns[:, :, 4], -1, -2) + from_y)
    return (diag_density, x_density, y_density)

def reference(diag_blocks, x_coupling, y_coupling, levels, listed):
    identity = jnp.eye(BLK, dtype=jnp.float32)
    pos_x = jnp.arange(NX, dtype=jnp.int32)[:, None]
    pos_y = jnp.arange(NY, dtype=jnp.int32)[None, :]
    flag_x = listed[:, :, 0].astype(jnp.float32) * (pos_x < NX - 1).astype(jnp.float32)
    flag_y = listed[:, :, 1].astype(jnp.float32) * (pos_y < NY - 1).astype(jnp.float32)
    onsite = 0.5 * (diag_blocks + jnp.swapaxes(diag_blocks, -1, -2)) + levels[..., None] * identity
    coup_x = x_coupling * flag_x[:, :, None, None]
    coup_y = y_coupling * flag_y[:, :, None, None]
    diag_one, x_one, y_one = sweep(onsite, coup_x, coup_y)
    onsite_two = onsite + hubbard * (diag_one - 0.5 * identity)
    coup_x_two = coup_x + hubbard * x_one
    coup_y_two = coup_y + hubbard * y_one
    diag_two, x_two, y_two = sweep(onsite_two, coup_x_two, coup_y_two)
    return (diag_two, x_two, y_two)
```

```python
import functools

import jax
import jax.numpy as jnp
from jax import lax
from jax.experimental import pallas as pl
from jax.experimental.pallas import tpu as pltpu
from jax.sharding import PartitionSpec as P

hubbard = 1.0
MESH = pl.DeviceIdType.MESH
F32 = jnp.float32
BF16 = jnp.bfloat16
TILE = 256


def mm(a, b):
    return jnp.dot(a, b, preferred_element_type=F32)


def grid2(rows, cols):
    return (
        lax.broadcasted_iota(jnp.int32, (rows, cols), 0),
        lax.broadcasted_iota(jnp.int32, (rows, cols), 1),
    )


def eye(w):
    r, c = grid2(w, w)
    return r == c


def when(cond, run):
    if cond is True:
        run()
    elif cond is not False:
        pl.when(cond)(run)


def pack(block, ref, flags):
    w = block.shape[0]
    h = w // 2
    r, c = grid2(h, w)
    low = block[h:, :]
    ref[:h, :] = jnp.where((c < h) & (c > r), pltpu.roll(low, h, 1), block[:h, :])
    row = jnp.sum(jnp.where(c == r + h, low, 0.0), axis=0, keepdims=True)
    lane = lax.broadcasted_iota(jnp.int32, (1, w), 1)
    for at, flag in enumerate(flags):
        row = jnp.where(lane == at, flag, row)
    ref[h:, :] = jnp.broadcast_to(row, (8, w))


def unpack(ref):
    w = ref.shape[1]
    h = w // 2
    r, c = grid2(w, w)
    top = ref[:h, :]
    both = jnp.concatenate([top, pltpu.roll(top, h, 1)], axis=0)
    keep = ((r < h) & ((c >= h) | (r >= c))) | ((r >= h) & (c > r))
    block = jnp.where(keep, both, both.T)
    return jnp.where((r == c) & (r >= h), jnp.broadcast_to(ref[h : h + 1, :], (w, w)), block)


def sweep(w, n, a, s, x, rf, emit):
    def bl(i):
        return slice(i * w, (i + 1) * w)

    s[...] = mm(a[...], a[...]).astype(BF16)
    x[0] = mm(a[:w, :], s[...])
    total = jnp.zeros((1, w), F32)
    for step, r0 in enumerate(range(0, n, TILE)):
        r1 = min(r0 + TILE, n)
        f = mm(s[r0:r1, :], s[:, r0:])
        f = jnp.sum(f * f, axis=0, keepdims=True)
        for c0 in range(0, n - r0, w):
            part = f[:, c0 : c0 + w]
            total = total + (part if c0 < r1 - r0 else 2.0 * part)
        if step == 0:
            x[1] = mm(x[0].astype(BF16), s[...])
        if step == 1:
            x[2] = mm(x[1].astype(BF16), s[...])
    x[3] = mm(x[2].astype(BF16), s[...])
    squares = jnp.sum(total, axis=1, keepdims=True)
    scale_two = jnp.sqrt(jnp.sqrt(squares + 1e-06))
    scale_one = jnp.sqrt(scale_two)
    al = 1.5 / scale_one
    be = 0.5 / (scale_one * scale_two)
    coef = [
        -0.75 * al,
        0.75 * be + 0.25 * al * al * al,
        -0.75 * al * al * be,
        0.75 * al * be * be,
        -0.25 * be * be * be,
    ]

    def column(i):
        value = coef[0] * rf[i]
        for p in range(4):
            value = value + coef[1 + p] * x[p, :, bl(i)]
        return value

    emit(column)


def kernel(
    sizes, nb, diag_hbm, x_hbm, y_hbm, lev_hbm, list_hbm, out_ref,
    din, lin, fin, in_sems,
    own, rb1, sp1, rp1, sp2, rp2, rc2, rf3,
    a, s, x, rf, bf, ct1, ct2, tr3,
    send_sems, recv_sems,
):
    nx, ny = sizes
    w = din.shape[0]
    n = (1 + nb) * w
    ix = lax.axis_index("space")
    iy = lax.axis_index("grp")
    lower, upper = jnp.maximum(ix - 1, 0), jnp.minimum(ix + 1, nx - 1)
    has = [ix > 0, ix < nx - 1]
    ups = [False, has[1]]
    downs = [has[0], False]
    dev = [(lower, iy), (upper, iy)]
    opp = [1, 0]
    if nb == 3:
        has += [True]
        ups += [iy == 0]
        downs += [iy == 1]
        dev += [(ix, 1 - iy)]
        opp += [2]
    else:
        has += [iy > 0, iy < ny - 1]
        ups += [False, has[3]]
        downs += [has[2], False]
        dev += [(ix, jnp.maximum(iy - 1, 0)), (ix, jnp.minimum(iy + 1, ny - 1))]
        opp += [3, 2]
    slots = range(nb)
    axis_of = [0, 0, 1, 1]
    coup_hbm = [x_hbm, y_hbm]

    def bl(i):
        return slice(i * w, (i + 1) * w)

    barrier = pltpu.get_barrier_semaphore()
    count = 0
    for k in slots:
        def greet(k=k):
            pl.semaphore_signal(barrier, inc=1, device_id=dev[k], device_id_type=MESH)

        when(has[k], greet)
        count = count + (1 if has[k] is True else has[k].astype(jnp.int32))

    loads = [
        pltpu.make_async_copy(diag_hbm.at[0, 0], din, in_sems.at[0]),
        pltpu.make_async_copy(lev_hbm.at[0], lin, in_sems.at[1]),
        pltpu.make_async_copy(list_hbm.at[0], fin, in_sems.at[2]),
        pltpu.make_async_copy(x_hbm.at[0, 0], own.at[0], in_sems.at[3]),
        pltpu.make_async_copy(y_hbm.at[0, 0], own.at[1], in_sems.at[4]),
    ]
    for load in loads:
        load.start()

    def transfer(kind, k, src, dst):
        return pltpu.make_async_remote_copy(
            src_ref=src, dst_ref=dst.at[opp[k]], send_sem=send_sems.at[kind, k],
            recv_sem=recv_sems.at[kind, opp[k]], device_id=dev[k], device_id_type=MESH,
        )

    def coup1(k):
        return transfer(0, k, coup_hbm[axis_of[k]].at[0, 0], rb1)

    def diag1(k):
        return transfer(1, k, sp1, rp1)

    def coup2(k):
        return transfer(2, k, ct1.at[1 + k], rc2)

    def diag2(k):
        return transfer(3, k, sp2, rp2)

    def coup3(k):
        return transfer(4, k, tr3.at[k], rf3)

    order = list(range(2, nb)) + [1, 0]

    zero = jnp.zeros((w, w), F32)
    for k in slots:
        def clear(k=k):
            rp1[k] = jnp.zeros((w // 2 + 8, w), F32)
            rp2[k] = jnp.zeros((w // 2 + 8, w), F32)
            rc2[k] = zero

        if has[k] is not True:
            when(jnp.logical_not(has[k]), clear)
        if downs[k] is not False:
            def clear_down(k=k):
                rb1[k] = zero

            when(jnp.logical_not(downs[k]), clear_down)
        if ups[k] is not False:
            def clear_up(k=k):
                rf3[k] = zero

            when(jnp.logical_not(ups[k]), clear_up)
    a[...] = jnp.zeros((n, n), BF16)

    pl.semaphore_wait(barrier, count)
    for k in order:
        when(ups[k], lambda k=k: coup1(k).start())
    for load in loads:
        load.wait()

    one_eye = eye(w)
    flags = [
        fin[0, 0].astype(F32) * (ix < nx - 1).astype(F32),
        fin[0, 1].astype(F32) * (iy < ny - 1).astype(F32),
    ]
    raw = din[...]
    onsite = 0.5 * (raw + raw.T) + jnp.where(one_eye, jnp.broadcast_to(lin[...], (w, w)), 0.0)
    pack(onsite, sp1, flags)
    for k in order:
        when(has[k], lambda k=k: diag1(k).start())

    rf[0] = onsite
    a[bl(0), bl(0)] = onsite.astype(BF16)

    def place(k, row, col):
        rf[1 + k] = row
        bf[k] = col
        a[bl(0), bl(1 + k)] = row.astype(BF16)
        a[bl(1 + k), bl(0)] = col.astype(BF16)

    for k in slots:
        if downs[k] is False:
            mine = own[axis_of[k]] * flags[axis_of[k]]
            place(k, mine, mine.T)
    arrival = [1, 0] + list(range(2, nb))
    for k in arrival:
        when(downs[k], lambda k=k: coup1(opp[k]).wait_recv())
        if downs[k] is not False:
            got = rb1[k]
            if ups[k] is not False:
                got = jnp.where(ups[k], own[axis_of[k]], got)
            bf[k] = got
            rf[1 + k] = got.T
    for k in arrival:
        when(has[k], lambda k=k: diag1(opp[k]).wait_recv())
        a[bl(1 + k), bl(1 + k)] = unpack(rp1.at[k]).astype(BF16)
        if downs[k] is not False:
            at = axis_of[k]
            flag = rp1[k, w // 2 : w // 2 + 1, at : at + 1]
            col, row = bf[k], rf[1 + k]
            if ups[k] is not False:
                flag = jnp.where(ups[k], flags[at], flag)
                col, row = jnp.where(ups[k], row, col), jnp.where(ups[k], col, row)
            place(k, row * flag, col * flag)

    def emit_one(column):
        for k in order:
            ct1[1 + k] = column(1 + k)
            when(has[k], lambda k=k: coup2(k).start())
        c0 = column(0)
        two = rf[0] + hubbard * (0.5 * (c0 + c0.T))
        pack(two, sp2, [])
        for k in order:
            when(has[k], lambda k=k: diag2(k).start())
        rf[0] = two
        a[bl(0), bl(0)] = two.astype(BF16)
        for k in slots:
            bf[k] = bf[k] + 0.5 * hubbard * ct1[1 + k].T

    sweep(w, n, a, s, x, rf, emit_one)

    for k in arrival:
        when(has[k], lambda k=k: coup2(opp[k]).wait_recv())
        col = bf[k] + 0.5 * hubbard * rc2[k]
        place(k, col.T, col)
    for k in arrival:
        when(has[k], lambda k=k: diag2(opp[k]).wait_recv())
        a[bl(1 + k), bl(1 + k)] = unpack(rp2.at[k]).astype(BF16)

    halves = [None, None]

    def emit_two(column):
        for k in order:
            ct = column(1 + k)
            if downs[k] is not False:
                tr3[k] = ct.T
                when(downs[k], lambda k=k: coup3(k).start())
            if ups[k] is not False:
                half = 0.5 * ct
                if downs[k] is not False:
                    half = jnp.where(ups[k], half, 0.0)
                out_ref[1 + axis_of[k]] = half
        c0 = column(0)
        out_ref[0] = 0.5 * (c0 + c0.T) + jnp.where(one_eye, 0.5, 0.0)

    sweep(w, n, a, s, x, rf, emit_two)

    for k in reversed(order):
        if ups[k] is not False:
            when(ups[k], lambda k=k: coup3(opp[k]).wait_recv())
            out_ref[1 + axis_of[k]] = out_ref[1 + axis_of[k]] + 0.5 * rf3[k]
    for k in slots:
        def drain(k=k):
            diag1(k).wait_send()
            coup2(k).wait_send()
            diag2(k).wait_send()

        when(has[k], drain)
        when(ups[k], lambda k=k: coup1(k).wait_send())
        when(downs[k], lambda k=k: coup3(k).wait_send())


def write_out(in_ref, od_ref, ox_ref, oy_ref, sems):
    copies = [
        pltpu.make_async_copy(in_ref.at[i], ref.at[0, 0], sems.at[i])
        for i, ref in enumerate((od_ref, ox_ref, oy_ref))
    ]
    for copy in copies:
        copy.start()
    for copy in copies:
        copy.wait()


def per_device(diag_blocks, x_coupling, y_coupling, levels, listed):
    w = diag_blocks.shape[-1]
    sizes = (lax.axis_size("space"), lax.axis_size("grp"))
    nb = 3 if sizes[1] == 2 else 4
    n = (1 + nb) * w
    block = jax.ShapeDtypeStruct((1, 1, w, w), F32)
    any_spec = pl.BlockSpec(memory_space=pl.ANY)
    vmem_spec = pl.BlockSpec(memory_space=pltpu.VMEM)
    half = w // 2 + 8
    results = pl.pallas_call(
        functools.partial(kernel, sizes, nb),
        out_shape=pltpu.VMEM((3, w, w), F32),
        in_specs=[any_spec] * 5,
        out_specs=vmem_spec,
        scratch_shapes=[
            pltpu.VMEM((w, w), F32),
            pltpu.VMEM((1, w), F32),
            pltpu.SMEM((1, 2), jnp.int32),
            pltpu.SemaphoreType.DMA((5,)),
            pltpu.VMEM((2, w, w), F32),
            pltpu.VMEM((nb, w, w), F32),
            pltpu.VMEM((half, w), F32),
            pltpu.VMEM((nb, half, w), F32),
            pltpu.VMEM((half, w), F32),
            pltpu.VMEM((nb, half, w), F32),
            pltpu.VMEM((nb, w, w), F32),
            pltpu.VMEM((nb, w, w), F32),
            pltpu.VMEM((n, n), BF16),
            pltpu.VMEM((n, n), BF16),
            pltpu.VMEM((4, w, n), F32),
            pltpu.VMEM((1 + nb, w, w), F32),
            pltpu.VMEM((nb, w, w), F32),
            pltpu.VMEM((1 + nb, w, w), F32),
            pltpu.VMEM((1 + nb, w, w), F32),
            pltpu.VMEM((nb, w, w), F32),
            pltpu.SemaphoreType.DMA((5, nb)),
            pltpu.SemaphoreType.DMA((5, nb)),
        ],
        compiler_params=pltpu.CompilerParams(collective_id=0, has_side_effects=True),
    )(diag_blocks, x_coupling, y_coupling, levels, listed)
    return pl.pallas_call(
        write_out,
        out_shape=(block, block, block),
        in_specs=[vmem_spec],
        out_specs=(any_spec,) * 3,
        scratch_shapes=[pltpu.SemaphoreType.DMA((3,))],
    )(pltpu.with_memory_space_constraint(results, pltpu.VMEM))


def solution(mesh):
    blocks = P("space", "grp", None, None)
    rows = P("space", "grp", None)
    return jax.shard_map(
        per_device,
        mesh=mesh,
        in_specs=(blocks, blocks, blocks, rows, rows),
        out_specs=(blocks, blocks, blocks),
        check_vma=False,
    )
```
